32 devices in a mesh: col: 8 (over y, x, core), dev: 4 (over z).
Axes of the slice: x: 2, y: 2, z: 4, core: 2. Of those that a mesh axis runs over, the one named last changes fastest.
Arguments:
- first_factor: bfloat16 [16, 1024, 2048], P(None, 'col', 'dev'), may hold values from -1 to 1
- second_factor: bfloat16 [16, 1024, 2048], P(None, 'dev', 'col'), may hold values from -1 to 1
- amplitudes: bfloat16 [512, 1024, 1024], P(None, 'col', 'dev'), may hold values from -0.0059814453 to 0.0059814453
Outputs:
- ladder: float32 [512, 256], P(('col', 'dev'))
The draws below stay inside these ranges and needn't reach their ends.
All inputs are finite; a program needn't handle non-finite values.
Results may differ from the reference program's by a relative error of at most 0.0029.
Values may be sent and summed in bfloat16 or wider, within the bound.
A program may use at most 128 MiB of HBM per device.

```python
import jax
import jax.numpy as jnp
from jax import lax

V = 1024
Q = 2048
P_SIZE = 512
WA = 16
WB = 16


def with_spikes(entries, key, source, target, shards_of, factor):
    owner, partner = [(jnp.arange(entries.shape[position]) // (entries.shape[position] // shards_of)).reshape([-1 if axis == position else 1 for axis in range(entries.ndim)]) for position in (source, target)]
    chosen = jax.random.permutation(key, shards_of)[partner]
    strong = (owner == chosen) | (owner == (partner + shards_of // 2) % shards_of)
    return jnp.where(strong, factor * entries, entries)


def block_scale(stream_key, dims, pieces, low, top_value):
    def one(position, shards_of):
        heights = jax.random.uniform(jax.random.fold_in(jax.random.fold_in(stream_key, 6), position), (shards_of,), jnp.float32, low / len(pieces), top_value / len(pieces))
        return jnp.repeat(jnp.exp(heights), dims[position] // shards_of).reshape((-1,) + (1,) * (len(dims) - position - 1))

    gain = one(*pieces[0])
    for cut in pieces[1:]:
        gain = gain * one(*cut)
    return gain


def gaussian(own_key, extent, scale, most, cuts=(), kind=jnp.bfloat16):
    array = jax.random.normal(own_key, extent, jnp.float32) * scale
    if len(cuts) > 0:
        array = block_scale(own_key, extent, cuts, -0.22, 0.18) * array
    return jnp.clip(array, min=-most, max=most).astype(kind)


def bell_draw_with(own_key, shape, spread, reach, cuts, heavy, kind=jnp.bfloat16):
    array = spread * jax.random.normal(own_key, shape, jnp.float32)
    if cuts:
        array = array * block_scale(own_key, shape, cuts, -0.22, 0.18)
    return jnp.clip(with_spikes(array, jax.random.fold_in(own_key, 3), *heavy), -reach, reach).astype(kind)


def setup_inputs(seed: int = 0) -> dict:
    arg_keys = jax.random.split(jax.random.key(seed), 4)
    first_factor = gaussian(arg_keys[0], (WA, V, Q), 0.1487, 1.0, ((1, 8), (2, 4)))
    second_factor = gaussian(arg_keys[1], (WB, V, Q), 0.1487, 1.0, ((1, 4), (2, 8)))
    amplitudes = bell_draw_with(arg_keys[2], (P_SIZE, V, V), 0.0009765625, 0.0059814453, ((1, 8), (2, 4)), (1, 0, 8, 2.0))
    return dict(first_factor=first_factor, second_factor=second_factor, amplitudes=amplitudes)


def reference(first_factor, second_factor, amplitudes):
    second_flat = second_factor.reshape(WB * V, Q)
    amp_flat = amplitudes.reshape(P_SIZE, V * V)

    def one_row(first_row):
        tile = jnp.dot(first_row, second_flat.T, preferred_element_type=jnp.float32).astype(jnp.bfloat16)
        tile = tile.reshape(V, WB, V).transpose(1, 0, 2).reshape(WB, V * V)
        return jnp.dot(amp_flat, tile.T, preferred_element_type=jnp.float32)

    rows = lax.map(one_row, first_factor)
    return rows.transpose(1, 0, 2).reshape(P_SIZE, WA * WB)
```

```python
import functools

import jax
import jax.numpy as jnp
from jax import lax
from jax.experimental import pallas as pl
from jax.experimental.pallas import tpu as pltpu
from jax.sharding import PartitionSpec as P

MESH = pl.DeviceIdType.MESH
BLOCK = 16
GROUP = 8
WIDE = 8
EARLY = 3
NT = (((1,), (1,)), ((), ()))


def kernel(
    ncol, ndev, first, second, amps, out,
    first_all, second_all, held, tile, total, parts, final, half_sum,
    f_sem, own_sem, z_send, z_recv, r_send, r_recv, c_send, c_recv, t_sem, s_send, s_recv, d_send, d_recv,
):
    col, dev = lax.axis_index("col"), lax.axis_index("dev")
    n_a, n_c, q_first = first.shape
    n_b, n_d, q_second = second.shape
    groups = amps.shape[0]
    pairs = groups * BLOCK
    size = n_a
    chunks = n_c // size
    chips = ncol // 2
    far = chips // 2
    core, chip = lax.rem(col, 2), col // 2

    def swap(spot):
        return jnp.where(spot < far, spot, 3 * far - 1 - spot)

    spot = swap(chip)

    def at_spot(offset):
        return swap(lax.rem(spot + offset + 2 * chips, chips)) * 2 + core

    partner = chip * 2 + 1 - core
    own_q = pl.ds(pl.multiple_of(dev * q_first, q_first), q_first)

    barrier = pltpu.get_barrier_semaphore()
    for off in range(1, ncol):
        pl.semaphore_signal(
            barrier, inc=1, device_id={"col": lax.rem(col + off, ncol)}, device_id_type=MESH
        )
    for off in range(1, ndev):
        pl.semaphore_signal(
            barrier, inc=1, device_id={"dev": lax.rem(dev + off, ndev)}, device_id_type=MESH
        )

    def f_copy(k):
        return pltpu.make_async_copy(
            first.at[:, pl.ds(pl.multiple_of(k * size, size), size), :],
            first_all.at[pl.ds(k * size, size), :, own_q],
            f_sem.at[k],
        )

    def t_copy(k):
        return pltpu.make_async_copy(
            amps.at[:, :, pl.ds(pl.multiple_of(k * BLOCK, BLOCK), BLOCK), :], held.at[k],
            t_sem.at[k],
        )

    own_second = pltpu.make_async_copy(
        second, second_all.at[:, :, pl.ds(pl.multiple_of(col * q_second, q_second), q_second)],
        own_sem.at[0],
    )

    def z_slice(source, k):
        return first_all.at[
            pl.ds(k * size, size), :, pl.ds(pl.multiple_of(source * q_first, q_first), q_first)
        ]

    def z_copy(way, hop, k):
        step = 1 if way == 0 else -1
        here = z_slice(dev - step * (hop - 1), k)
        return pltpu.make_async_remote_copy(
            src_ref=here,
            dst_ref=here,
            send_sem=z_send.at[way, hop - 1, k],
            recv_sem=z_recv.at[way, hop - 1, k],
            device_id={"dev": dev + step},
            device_id_type=MESH,
        )

    def z_arrival(way, hop, k):
        step = 1 if way == 0 else -1
        here = z_slice(dev - step * hop, k)
        return pltpu.make_async_copy(here, here, z_recv.at[way, hop - 1, k])

    def sends(way, hop):
        if way == 0:
            return (dev - (hop - 1) >= 0) & (dev + 1 < ndev)
        return (dev + (hop - 1) < ndev) & (dev - 1 >= 0)

    def receives(way, hop):
        return (dev - hop >= 0) if way == 0 else (dev + hop < ndev)

    def z_own(k):
        for way in range(2):
            @pl.when(sends(way, 1))
            def _():
                z_copy(way, 1, k).start()

    def z_relay(hop, k):
        for way in range(2):
            @pl.when(receives(way, hop) & sends(way, hop + 1))
            def _():
                z_arrival(way, hop, k).wait()
                z_copy(way, hop + 1, k).start()

    def z_need(k):
        for way in range(2):
            for hop in range(1, ndev):
                kept = receives(way, hop)
                if hop + 1 < ndev:
                    kept &= jnp.logical_not(sends(way, hop + 1))

                @pl.when(kept)
                def _():
                    z_arrival(way, hop, k).wait()

    wide = n_b // 2

    def p_slice(source, h):
        return second_all.at[
            pl.ds(h * wide, wide), :, pl.ds(pl.multiple_of(source * q_second, q_second), q_second)
        ]

    def p_source(way, hop):
        return at_spot(-hop if way == 0 else hop)

    def r_copy(way, hop, h):
        source = p_source(way, hop - 1)
        src = second.at[pl.ds(h * wide, wide)] if hop == 1 else p_slice(source, h)
        return pltpu.make_async_remote_copy(
            src_ref=src,
            dst_ref=p_slice(source, h),
            send_sem=r_send.at[way, hop - 1, h],
            recv_sem=r_recv.at[way, hop - 1, h],
            device_id={"col": at_spot(1 if way == 0 else -1)},
            device_id_type=MESH,
        )

    def r_arrival(way, hop, h):
        here = p_slice(p_source(way, hop), h)
        return pltpu.make_async_copy(here, here, r_recv.at[way, hop - 1, h])

    def c_copy(way, hop, h):
        source = p_source(way, hop)
        src = second.at[pl.ds(h * wide, wide)] if hop == 0 else p_slice(source, h)
        return pltpu.make_async_remote_copy(
            src_ref=src,
            dst_ref=p_slice(source, h),
            send_sem=c_send.at[way, hop, h],
            recv_sem=c_recv.at[way, hop, h],
            device_id={"col": partner},
            device_id_type=MESH,
        )

    def c_arrival(way, hop, h):
        source = p_source(way, hop) + 1 - 2 * core
        here = p_slice(source, h)
        return pltpu.make_async_copy(here, here, c_recv.at[way, hop, h])

    def travels(way, hop):
        if hop < far:
            return (0, 1) if way == 0 else (1, 0)
        return (way,) if hop == far else ()

    pieces = [
        (way, hop, travels(way, hop)[place])
        for hop in range(1, far + 1)
        for place in range(len(travels(0, hop)))
        for way in range(2)
    ]
    shared = [(0, 0, 0), (0, 0, 1)] + pieces

    def take(way, hop, h):
        r_arrival(way, hop, h).wait()
        if h in travels(way, hop + 1):
            r_copy(way, hop + 1, h).start()
        c_copy(way, hop, h).start()

    def turn_first(k):
        f_copy(k).wait()
        rows = pl.ds(k * size, size)
        first_all[rows, :, own_q] = jnp.swapaxes(first_all[rows, :, own_q], 0, 1)

    def turn_block(k):
        t_copy(k).wait()

        def turn(i, _):
            held[k, i] = jnp.swapaxes(held[k, i], 0, 1)
            return 0

        lax.fori_loop(0, groups, turn, 0)

    for k in range(chunks):
        f_copy(k).start()
    own_second.start()
    pl.semaphore_wait(barrier, ncol + ndev - 2)
    for way, hop, h in pieces:
        if hop == 1:
            r_copy(way, 1, h).start()
    for h in range(2):
        c_copy(0, 0, h).start()
    for k in range(chunks):
        turn_first(k)
        z_own(k)
        t_copy(k).start()

    parts_of = {}
    for number, piece in enumerate(pieces):
        parts_of.setdefault(min(chunks - 1, (number // 2 + 1) * chunks // 2 - 1), []).append(piece)
    for k in range(chunks):
        turn_block(k)
        z_relay(1, k)
        if k < chunks - 1:
            for piece in parts_of.get(k, []):
                take(*piece)
    late = parts_of.get(chunks - 1, [])
    for piece in late[:2]:
        take(*piece)
    for k in range(min(EARLY, chunks)):
        for hop in range(2, ndev - 1):
            z_relay(hop, k)
    for piece in late[2:]:
        take(*piece)
    own_second.wait()
    for piece in shared:
        c_arrival(*piece).wait()

    total[...] = jnp.zeros_like(total)

    def one_block(k, _):
        z_need(k)

        def one_b(b, _):
            left = first_all[pl.ds(k * size, size)].reshape(size * n_a, -1)
            right = second_all[pl.ds(b * WIDE, WIDE)].reshape(WIDE * n_d, -1)
            got = lax.dot_general(left, right, NT, preferred_element_type=jnp.float32)
            got = got.astype(jnp.bfloat16)
            for i in range(WIDE):
                tile[:, b * WIDE + i] = got[:, i * n_d : (i + 1) * n_d].reshape(size, n_a, n_d)
            return 0

        lax.fori_loop(0, n_b // WIDE, one_b, 0)

        @pl.when(k + EARLY < chunks)
        def _():
            for hop in range(2, ndev - 1):
                z_relay(hop, k + EARLY)

        def some_c(g, _):
            group = [g * GROUP + i for i in range(GROUP)]
            left = jnp.concatenate([held[k, :, c].reshape(pairs, n_d) for c in group], axis=1)
            right = jnp.concatenate([tile[c].reshape(n_b * n_a, n_d) for c in group], axis=1)
            total[...] += lax.dot_general(left, right, NT, preferred_element_type=jnp.float32)
            return 0

        lax.fori_loop(0, size // GROUP, some_c, 0)
        return 0

    lax.fori_loop(0, chunks, one_block, 0)

    some = pairs // ncol

    def s_copy(off):
        to = lax.rem(col + off, ncol)
        return pltpu.make_async_remote_copy(
            src_ref=total.at[pl.ds(pl.multiple_of(to * some, some), some)],
            dst_ref=parts.at[off],
            send_sem=s_send.at[off],
            recv_sem=s_recv.at[off],
            device_id={"col": to},
            device_id_type=MESH,
        )

    for off in range(1, ncol):
        s_copy(off).start()
    mine = total[pl.ds(pl.multiple_of(col * some, some), some), :]
    for off in range(1, ncol):
        s_copy(off).wait_recv()
        mine += parts[off]
    half_sum[...] = mine.reshape(half_sum.shape)

    def d_copy(off):
        to = lax.rem(dev + off, ndev)
        return pltpu.make_async_remote_copy(
            src_ref=half_sum.at[to],
            dst_ref=final.at[off],
            send_sem=d_send.at[off],
            recv_sem=d_recv.at[off],
            device_id={"dev": to},
            device_id_type=MESH,
        )

    for off in range(1, ndev):
        d_copy(off).start()
    width = n_a * n_b
    rows = lax.broadcasted_iota(jnp.int32, (width, width), 0)
    columns = lax.broadcasted_iota(jnp.int32, (width, width), 1)
    order = (rows == lax.rem(columns, n_b) * n_a + lax.div(columns, n_b)).astype(jnp.float32)
    result = half_sum[dev]
    for off in range(1, ndev):
        d_copy(off).wait_recv()
        result += final[off]
    out[...] = jnp.dot(
        result, order, precision=lax.Precision.HIGHEST, preferred_element_type=jnp.float32
    )

    for off in range(1, ncol):
        s_copy(off).wait_send()
    for off in range(1, ndev):
        d_copy(off).wait_send()
    for piece in pieces:
        r_copy(*piece).wait_send()
    for piece in shared:
        c_copy(*piece).wait_send()

    def drain(k, _):
        for way in range(2):
            for hop in range(1, ndev):
                @pl.when(sends(way, hop))
                def _():
                    z_copy(way, hop, k).wait_send()
        return 0

    lax.fori_loop(0, chunks, drain, 0)


def on_device(ncol, ndev, first_factor, second_factor, amplitudes):
    n_a, n_c, q_first = first_factor.shape
    n_b, n_d, q_second = second_factor.shape
    pairs = amplitudes.shape[0]
    groups = pairs // BLOCK
    size = n_a
    chunks = n_c // size
    far = ncol // 4
    whole = q_first * ndev
    some = pairs // ncol
    few = some // ndev
    width = n_a * n_b
    anywhere = pl.BlockSpec(memory_space=pl.ANY)
    dma = pltpu.SemaphoreType.DMA
    return pl.pallas_call(
        functools.partial(kernel, ncol, ndev),
        out_shape=jax.ShapeDtypeStruct((few, width), jnp.float32),
        in_specs=[anywhere] * 3,
        out_specs=pl.BlockSpec(memory_space=pltpu.VMEM),
        scratch_shapes=[
            pltpu.VMEM((n_c, n_a, whole), jnp.bfloat16),
            pltpu.VMEM((n_b, n_d, whole), jnp.bfloat16),
            pltpu.VMEM((n_c // BLOCK, groups, BLOCK, BLOCK, n_d), jnp.bfloat16),
            pltpu.VMEM((size, n_b, n_a, n_d), jnp.bfloat16),
            pltpu.VMEM((pairs, width), jnp.float32),
            pltpu.VMEM((ncol, some, width), jnp.float32),
            pltpu.VMEM((ndev, few, width), jnp.float32),
            pltpu.VMEM((ndev, few, width), jnp.float32),
            dma((chunks,)),
            dma((1,)),
            dma((2, ndev - 1, chunks)),
            dma((2, ndev - 1, chunks)),
            dma((2, far, 2)),
            dma((2, far, 2)),
            dma((2, far + 1, 2)),
            dma((2, far + 1, 2)),
            dma((n_c // BLOCK,)),
            dma((ncol,)),
            dma((ncol,)),
            dma((ndev,)),
            dma((ndev,)),
        ],
        compiler_params=pltpu.CompilerParams(
            collective_id=0, has_side_effects=True, vmem_limit_bytes=67043328
        ),
    )(first_factor, second_factor, amplitudes.reshape(groups, BLOCK, n_c, n_d))


def solution(mesh):
    placed = (P(None, "col", "dev"), P(None, "dev", "col"), P(None, "col", "dev"))
    return jax.shard_map(
        functools.partial(on_device, mesh.shape["col"], mesh.shape["dev"]),
        mesh=mesh, in_specs=placed, out_specs=P(("col", "dev"), None), check_vma=False,
    )
```

```python
import functools

import jax
import jax.numpy as jnp
from jax import lax
from jax.experimental import pallas as pl
from jax.experimental.pallas import tpu as pltpu
from jax.sharding import PartitionSpec as P

MESH = pl.DeviceIdType.MESH
BLOCK = 16
GROUP = 8
WIDE = 8
EARLY = 3
NT = (((1,), (1,)), ((), ()))


def kernel(
    ncol, ndev, first, second, amps, out,
    first_all, second_all, held, tile, carry, order, total, parts, final, half_sum,
    f_sem, own_sem, z_send, z_recv, r_send, r_recv, c_send, c_recv, t_sem, s_send, s_recv, d_send, d_recv,
):
    col, dev = lax.axis_index("col"), lax.axis_index("dev")
    n_a, n_c, q_first = first.shape
    n_b, n_d, q_second = second.shape
    groups = amps.shape[0]
    pairs = groups * BLOCK
    size = n_a
    chunks = n_c // size
    chips = ncol // 2
    far = chips // 2
    core, chip = lax.rem(col, 2), col // 2

    def swap(spot):
        return jnp.where(spot < far, spot, 3 * far - 1 - spot)

    spot = swap(chip)

    def at_spot(offset):
        return swap(lax.rem(spot + offset + 2 * chips, chips)) * 2 + core

    partner = chip * 2 + 1 - core
    own_q = pl.ds(pl.multiple_of(dev * q_first, q_first), q_first)

    barrier = pltpu.get_barrier_semaphore()
    for off in range(1, ncol):
        pl.semaphore_signal(
            barrier, inc=1, device_id={"col": lax.rem(col + off, ncol)}, device_id_type=MESH
        )
    for off in range(1, ndev):
        pl.semaphore_signal(
            barrier, inc=1, device_id={"dev": lax.rem(dev + off, ndev)}, device_id_type=MESH
        )

    def f_copy(k):
        return pltpu.make_async_copy(
            first.at[:, pl.ds(pl.multiple_of(k * size, size), size), :],
            first_all.at[pl.ds(k * size, size), :, own_q],
            f_sem.at[k],
        )

    def slot_of(k):
        return lax.rem(k, chunks - 1)

    def t_copy(k):
        return pltpu.make_async_copy(
            amps.at[:, :, pl.ds(pl.multiple_of(k * BLOCK, BLOCK), BLOCK), :],
            held.at[slot_of(k)],
            t_sem.at[k],
        )

    own_second = pltpu.make_async_copy(
        second, second_all.at[:, :, pl.ds(pl.multiple_of(col * q_second, q_second), q_second)],
        own_sem.at[0],
    )

    def z_slice(source, k):
        return first_all.at[
            pl.ds(k * size, size), :, pl.ds(pl.multiple_of(source * q_first, q_first), q_first)
        ]

    def z_copy(way, hop, k):
        step = 1 if way == 0 else -1
        here = z_slice(dev - step * (hop - 1), k)
        return pltpu.make_async_remote_copy(
            src_ref=here,
            dst_ref=here,
            send_sem=z_send.at[way, hop - 1, k],
            recv_sem=z_recv.at[way, hop - 1, k],
            device_id={"dev": dev + step},
            device_id_type=MESH,
        )

    def z_arrival(way, hop, k):
        step = 1 if way == 0 else -1
        here = z_slice(dev - step * hop, k)
        return pltpu.make_async_copy(here, here, z_recv.at[way, hop - 1, k])

    def sends(way, hop):
        if way == 0:
            return (dev - (hop - 1) >= 0) & (dev + 1 < ndev)
        return (dev + (hop - 1) < ndev) & (dev - 1 >= 0)

    def receives(way, hop):
        return (dev - hop >= 0) if way == 0 else (dev + hop < ndev)

    def z_own(k):
        for way in range(2):
            @pl.when(sends(way, 1))
            def _():
                z_copy(way, 1, k).start()

    def lone(way):
        return (dev == 1) if way == 0 else (dev == ndev - 2)

    def z_relay(hop, k, alone=None):
        for way in range(2):
            meant = receives(way, hop) & sends(way, hop + 1)
            if alone is not None:
                meant &= lone(way) == alone

            @pl.when(meant)
            def _():
                z_arrival(way, hop, k).wait()
                z_copy(way, hop + 1, k).start()

    def z_need(k, hops):
        for way in range(2):
            for hop in hops:
                kept = receives(way, hop)
                if hop + 1 < ndev:
                    kept &= jnp.logical_not(sends(way, hop + 1))

                @pl.when(kept)
                def _():
                    z_arrival(way, hop, k).wait()

    wide = n_b // 2

    def p_slice(source, h):
        return second_all.at[
            pl.ds(h * wide, wide), :, pl.ds(pl.multiple_of(source * q_second, q_second), q_second)
        ]

    def p_source(way, hop):
        return at_spot(-hop if way == 0 else hop)

    def r_copy(way, hop, h):
        source = p_source(way, hop - 1)
        src = second.at[pl.ds(h * wide, wide)] if hop == 1 else p_slice(source, h)
        return pltpu.make_async_remote_copy(
            src_ref=src,
            dst_ref=p_slice(source, h),
            send_sem=r_send.at[way, hop - 1, h],
            recv_sem=r_recv.at[way, hop - 1, h],
            device_id={"col": at_spot(1 if way == 0 else -1)},
            device_id_type=MESH,
        )

    def r_arrival(way, hop, h):
        here = p_slice(p_source(way, hop), h)
        return pltpu.make_async_copy(here, here, r_recv.at[way, hop - 1, h])

    def c_copy(way, hop, h):
        source = p_source(way, hop)
        src = second.at[pl.ds(h * wide, wide)] if hop == 0 else p_slice(source, h)
        return pltpu.make_async_remote_copy(
            src_ref=src,
            dst_ref=p_slice(source, h),
            send_sem=c_send.at[way, hop, h],
            recv_sem=c_recv.at[way, hop, h],
            device_id={"col": partner},
            device_id_type=MESH,
        )

    def c_arrival(way, hop, h):
        source = p_source(way, hop) + 1 - 2 * core
        here = p_slice(source, h)
        return pltpu.make_async_copy(here, here, c_recv.at[way, hop, h])

    def travels(way, hop):
        if hop < far:
            return (0, 1) if way == 0 else (1, 0)
        return (way,) if hop == far else ()

    pieces = [
        (way, hop, travels(way, hop)[place])
        for hop in range(1, far + 1)
        for place in range(len(travels(0, hop)))
        for way in range(2)
    ]
    shared = [(0, 0, 0), (0, 0, 1)] + pieces

    def take(way, hop, h):
        r_arrival(way, hop, h).wait()
        if h in travels(way, hop + 1):
            r_copy(way, hop + 1, h).start()
        c_copy(way, hop, h).start()

    def turn_first(k):
        f_copy(k).wait()
        rows = pl.ds(k * size, size)
        first_all[rows, :, own_q] = jnp.swapaxes(first_all[rows, :, own_q], 0, 1)

    def turn_block(k):
        t_copy(k).wait()
        slot = slot_of(k)

        def turn(i, _):
            held[slot, i] = jnp.swapaxes(held[slot, i], 0, 1)
            return 0

        lax.fori_loop(0, groups, turn, 0)

    for k in range(chunks):
        f_copy(k).start()
    own_second.start()
    pl.semaphore_wait(barrier, ncol + ndev - 2)
    for way, hop, h in pieces:
        if hop == 1:
            r_copy(way, 1, h).start()
    for h in range(2):
        c_copy(0, 0, h).start()
    ahead = chunks - 2
    for k in range(chunks):
        turn_first(k)
        if k < ahead:
            z_own(k)
    for k in range(chunks - 1):
        t_copy(k).start()

    width = n_a * n_b
    rows = lax.broadcasted_iota(jnp.int32, (width, width), 0)
    columns = lax.broadcasted_iota(jnp.int32, (width, width), 1)
    order[...] = (rows == lax.rem(columns, n_b) * n_a + lax.div(columns, n_b)).astype(jnp.bfloat16)

    def take_hop(want, place):
        for way in range(2):
            if place < len(travels(way, want)):
                take(way, want, travels(way, want)[place])

    def z_relays(k, hops):
        for hop in hops:
            z_relay(hop, k, False if hop == 1 else None)

    def z_prompt(blocks):
        if ndev > 2:
            for k in blocks:
                z_relay(1, k, True)

    further = range(2, ndev - 1)
    for k in range(min(2, chunks - 1)):
        turn_block(k)
        if ndev > 2:
            z_relay(1, k)
        z_own(ahead + k)
    for k in range(2, chunks - 1):
        turn_block(k)
    total[...] = jnp.zeros_like(total)
    half = 2 + (chunks - 2) // 2
    take_hop(1, 0)
    z_prompt(range(2, half))
    z_relays(0, further)
    take_hop(1, 1)
    z_prompt(range(half, chunks))
    z_relays(1, further)
    for k in range(2, EARLY):
        z_relays(k, range(1, ndev - 1))
    for hop in range(2, far + 1):
        for place in range(len(travels(0, hop))):
            take_hop(hop, place)
    own_second.wait()
    for piece in shared:
        c_arrival(*piece).wait()

    def rows_of(k):
        return pl.ds(k * size, size)

    def product(k, b, columns):
        left = first_all[rows_of(k), :, columns].reshape(size * n_a, -1)
        right = second_all[pl.ds(b * WIDE, WIDE), :, columns].reshape(WIDE * n_d, -1)
        return lax.dot_general(left, right, NT, preferred_element_type=jnp.float32)

    def keep(b, got):
        got = got.astype(jnp.bfloat16)
        for i in range(WIDE):
            tile[:, b * WIDE + i] = got[:, i * n_d : (i + 1) * n_d].reshape(size, n_a, n_d)

    def contract(k):
        slot = slot_of(k)

        def some_c(g, _):
            group = [g * GROUP + i for i in range(GROUP)]
            left = jnp.concatenate([held[slot, :, c].reshape(pairs, n_d) for c in group], axis=1)
            right = jnp.concatenate([tile[c].reshape(n_b * n_a, n_d) for c in group], axis=1)
            got = lax.dot_general(left, right, NT, preferred_element_type=jnp.float32)
            total[...] += got.reshape(total.shape)
            return 0

        lax.fori_loop(0, size // GROUP, some_c, 0)

    everything = pl.ds(0, ndev * q_first)

    def one_block(k, _):
        z_need(k, range(1, ndev))

        def one_b(b, _):
            keep(b, product(k, b, everything))
            return 0

        lax.fori_loop(0, n_b // WIDE, one_b, 0)

        @pl.when(k + EARLY < chunks)
        def _():
            z_relays(k + EARLY, range(1, ndev - 1))

        contract(k)

        @pl.when(k == 0)
        def _():
            t_copy(chunks - 1).start()

        @pl.when(k == 1)
        def _():
            turn_block(chunks - 1)

        return 0

    lax.fori_loop(0, chunks - 1, one_block, 0)

    end = chunks - 1
    low = dev * 2 < ndev
    last = pl.ds(pl.multiple_of(jnp.where(low, ndev - 1, 0) * q_first, q_first), q_first)
    others = pl.ds(pl.multiple_of(jnp.where(low, 0, q_first), q_first), (ndev - 1) * q_first)
    z_need(end, range(1, ndev - 1))

    def early_b(b, _):
        carry[b] = product(end, b, others)
        return 0

    lax.fori_loop(0, n_b // WIDE, early_b, 0)
    z_need(end, range(ndev - 1, ndev))

    def late_b(b, _):
        keep(b, carry[b] + product(end, b, last))
        return 0

    lax.fori_loop(0, n_b // WIDE, late_b, 0)
    contract(end)

    targets = [jnp.where(low, ndev - 1 - i, i) for i in range(ndev)]

    def s_copy(off, place):
        to, target = lax.rem(col + off, ncol), targets[place]
        return pltpu.make_async_remote_copy(
            src_ref=total.at[to, target],
            dst_ref=parts.at[off, target],
            send_sem=s_send.at[off, place],
            recv_sem=s_recv.at[off, place],
            device_id={"col": to},
            device_id_type=MESH,
        )

    def d_copy(target):
        return pltpu.make_async_remote_copy(
            src_ref=half_sum.at[target],
            dst_ref=final.at[dev],
            send_sem=d_send.at[target],
            recv_sem=d_recv.at[dev],
            device_id={"dev": target},
            device_id_type=MESH,
        )

    for place in range(ndev):
        for off in range(1, ncol):
            s_copy(off, place).start()
    for place in range(ndev):
        target = targets[place]
        mine = total[col, target]
        for off in range(1, ncol):
            s_copy(off, place).wait_recv()
            mine += parts[off, target]
        half_sum[target] = mine

        @pl.when(target != dev)
        def _():
            d_copy(target).start()

    result = half_sum[dev]
    for off in range(1, ndev):
        source = lax.rem(dev + off, ndev)
        pltpu.make_async_copy(final.at[source], final.at[source], d_recv.at[source]).wait()
        result += final[source]
    high = result.astype(jnp.bfloat16)
    result -= high.astype(jnp.float32)
    middle = result.astype(jnp.bfloat16)
    result -= middle.astype(jnp.float32)
    split = (high, middle, result.astype(jnp.bfloat16))
    moved = [jnp.dot(part, order[...], preferred_element_type=jnp.float32) for part in split]
    out[...] = moved[0] + moved[1] + moved[2]

    for place in range(ndev):
        for off in range(1, ncol):
            s_copy(off, place).wait_send()
    for off in range(1, ndev):
        d_copy(lax.rem(dev + off, ndev)).wait_send()
    for piece in pieces:
        r_copy(*piece).wait_send()
    for piece in shared:
        c_copy(*piece).wait_send()

    def drain(k, _):
        for way in range(2):
            for hop in range(1, ndev):
                @pl.when(sends(way, hop))
                def _():
                    z_copy(way, hop, k).wait_send()
        return 0

    lax.fori_loop(0, chunks, drain, 0)


def on_device(ncol, ndev, first_factor, second_factor, amplitudes):
    n_a, n_c, q_first = first_factor.shape
    n_b, n_d, q_second = second_factor.shape
    pairs = amplitudes.shape[0]
    groups = pairs // BLOCK
    size = n_a
    chunks = n_c // size
    far = ncol // 4
    whole = q_first * ndev
    some = pairs // ncol
    few = some // ndev
    width = n_a * n_b
    anywhere = pl.BlockSpec(memory_space=pl.ANY)
    dma = pltpu.SemaphoreType.DMA
    return pl.pallas_call(
        functools.partial(kernel, ncol, ndev),
        out_shape=jax.ShapeDtypeStruct((few, width), jnp.float32),
        in_specs=[anywhere] * 3,
        out_specs=pl.BlockSpec(memory_space=pltpu.VMEM),
        scratch_shapes=[
            pltpu.VMEM((n_c, n_a, whole), jnp.bfloat16),
            pltpu.VMEM((n_b, n_d, whole), jnp.bfloat16),
            pltpu.VMEM((n_c // BLOCK - 1, groups, BLOCK, BLOCK, n_d), jnp.bfloat16),
            pltpu.VMEM((size, n_b, n_a, n_d), jnp.bfloat16),
            pltpu.VMEM((n_b // WIDE, size * n_a, WIDE * n_d), jnp.float32),
            pltpu.VMEM((width, width), jnp.bfloat16),
            pltpu.VMEM((ncol, ndev, few, width), jnp.float32),
            pltpu.VMEM((ncol, ndev, few, width), jnp.float32),
            pltpu.VMEM((ndev, few, width), jnp.float32),
            pltpu.VMEM((ndev, few, width), jnp.float32),
            dma((chunks,)),
            dma((1,)),
            dma((2, ndev - 1, chunks)),
            dma((2, ndev - 1, chunks)),
            dma((2, far, 2)),
            dma((2, far, 2)),
            dma((2, far + 1, 2)),
            dma((2, far + 1, 2)),
            dma((n_c // BLOCK,)),
            dma((ncol, ndev)),
            dma((ncol, ndev)),
            dma((ndev,)),
            dma((ndev,)),
        ],
        compiler_params=pltpu.CompilerParams(
            collective_id=0, has_side_effects=True, vmem_limit_bytes=67043328
        ),
    )(first_factor, second_factor, amplitudes.reshape(groups, BLOCK, n_c, n_d))


def solution(mesh):
    placed = (P(None, "col", "dev"), P(None, "dev", "col"), P(None, "col", "dev"))
    return jax.shard_map(
        functools.partial(on_device, mesh.shape["col"], mesh.shape["dev"]),
        mesh=mesh, in_specs=placed, out_specs=P(("col", "dev"), None), check_vma=False,
    )
```

```python
import functools

import jax
import jax.numpy as jnp
from jax import lax
from jax.experimental import pallas as pl
from jax.experimental.pallas import tpu as pltpu
from jax.sharding import PartitionSpec as P

MESH = pl.DeviceIdType.MESH
BLOCK = 16
GROUP = 8
WIDE = 8
EARLY = 3
NT = (((1,), (1,)), ((), ()))


def kernel(
    ncol, ndev, first, second, amps, out,
    first_all, second_all, held, tile, carry, order, total, mate, joined, parts, final, half_sum,
    f_sem, own_sem, z_send, z_recv, r_send, r_recv, c_send, c_recv, t_sem, x_send, x_recv, s_send, s_recv, d_send, d_recv,
):
    col, dev = lax.axis_index("col"), lax.axis_index("dev")
    n_a, n_c, q_first = first.shape
    n_b, n_d, q_second = second.shape
    groups = amps.shape[0]
    pairs = groups * BLOCK
    size = n_a
    chunks = n_c // size
    chips = ncol // 2
    far = chips // 2
    core, chip = lax.rem(col, 2), col // 2

    def swap(spot):
        return jnp.where(spot < far, spot, 3 * far - 1 - spot)

    spot = swap(chip)

    def at_spot(offset):
        return swap(lax.rem(spot + offset + 2 * chips, chips)) * 2 + core

    partner = chip * 2 + 1 - core
    own_q = pl.ds(pl.multiple_of(dev * q_first, q_first), q_first)

    barrier = pltpu.get_barrier_semaphore()
    for off in range(1, ncol):
        pl.semaphore_signal(
            barrier, inc=1, device_id={"col": lax.rem(col + off, ncol)}, device_id_type=MESH
        )
    for off in range(1, ndev):
        pl.semaphore_signal(
            barrier, inc=1, device_id={"dev": lax.rem(dev + off, ndev)}, device_id_type=MESH
        )

    def f_copy(k):
        return pltpu.make_async_copy(
            first.at[:, pl.ds(pl.multiple_of(k * size, size), size), :],
            first_all.at[pl.ds(k * size, size), :, own_q],
            f_sem.at[k],
        )

    def slot_of(k):
        return lax.rem(k, chunks - 1)

    def t_copy(k):
        return pltpu.make_async_copy(
            amps.at[:, :, pl.ds(pl.multiple_of(k * BLOCK, BLOCK), BLOCK), :],
            held.at[slot_of(k)],
            t_sem.at[k],
        )

    own_second = pltpu.make_async_copy(
        second, second_all.at[:, :, pl.ds(pl.multiple_of(col * q_second, q_second), q_second)],
        own_sem.at[0],
    )

    def z_slice(source, k, share, shares):
        wide = q_first // shares
        start = pl.multiple_of(source * q_first + share * wide, wide)
        return first_all.at[pl.ds(k * size, size), :, pl.ds(start, wide)]

    def shares_of(hop):
        return 2 if hop == ndev - 1 else 1

    def z_copies(way, hop, k):
        step = 1 if way == 0 else -1
        source, shares = dev - step * (hop - 1), shares_of(hop)
        return [
            pltpu.make_async_remote_copy(
                src_ref=z_slice(source, k, share, shares),
                dst_ref=z_slice(source, k, share, shares),
                send_sem=z_send.at[way, hop - 1, k, share],
                recv_sem=z_recv.at[way, hop - 1, k, share],
                device_id={"dev": dev + step},
                device_id_type=MESH,
            )
            for share in range(shares)
        ]

    def z_arrivals(way, hop, k, chosen=(0, 1)):
        step = 1 if way == 0 else -1
        source, shares = dev - step * hop, shares_of(hop)
        here = {
            share: z_slice(source, k, share, shares) for share in range(shares) if share in chosen
        }
        return [
            pltpu.make_async_copy(ref, ref, z_recv.at[way, hop - 1, k, share])
            for share, ref in here.items()
        ]

    def sends(way, hop):
        if way == 0:
            return (dev - (hop - 1) >= 0) & (dev + 1 < ndev)
        return (dev + (hop - 1) < ndev) & (dev - 1 >= 0)

    def receives(way, hop):
        return (dev - hop >= 0) if way == 0 else (dev + hop < ndev)

    def z_own(k):
        for way in range(2):
            @pl.when(sends(way, 1))
            def _():
                for copy in z_copies(way, 1, k):
                    copy.start()

    def lone(way):
        return (dev == 1) if way == 0 else (dev == ndev - 2)

    def z_relay(hop, k, alone=None):
        for way in range(2):
            meant = receives(way, hop) & sends(way, hop + 1)
            if alone is not None:
                meant &= lone(way) == alone

            @pl.when(meant)
            def _():
                for arrival in z_arrivals(way, hop, k):
                    arrival.wait()
                for copy in z_copies(way, hop + 1, k):
                    copy.start()

    def z_need(k, hops, shares=(0, 1)):
        for way in range(2):
            for hop in hops:
                kept = receives(way, hop)
                if hop + 1 < ndev:
                    kept &= jnp.logical_not(sends(way, hop + 1))

                @pl.when(kept)
                def _():
                    for arrival in z_arrivals(way, hop, k, shares):
                        arrival.wait()

    wide = n_b // 2

    def p_slice(source, h):
        return second_all.at[
            pl.ds(h * wide, wide), :, pl.ds(pl.multiple_of(source * q_second, q_second), q_second)
        ]

    def p_source(way, hop):
        return at_spot(-hop if way == 0 else hop)

    def r_copy(way, hop, h):
        source = p_source(way, hop - 1)
        src = second.at[pl.ds(h * wide, wide)] if hop == 1 else p_slice(source, h)
        return pltpu.make_async_remote_copy(
            src_ref=src,
            dst_ref=p_slice(source, h),
            send_sem=r_send.at[way, hop - 1, h],
            recv_sem=r_recv.at[way, hop - 1, h],
            device_id={"col": at_spot(1 if way == 0 else -1)},
            device_id_type=MESH,
        )

    def r_arrival(way, hop, h):
        here = p_slice(p_source(way, hop), h)
        return pltpu.make_async_copy(here, here, r_recv.at[way, hop - 1, h])

    def c_copy(way, hop, h):
        source = p_source(way, hop)
        src = second.at[pl.ds(h * wide, wide)] if hop == 0 else p_slice(source, h)
        return pltpu.make_async_remote_copy(
            src_ref=src,
            dst_ref=p_slice(source, h),
            send_sem=c_send.at[way, hop, h],
            recv_sem=c_recv.at[way, hop, h],
            device_id={"col": partner},
            device_id_type=MESH,
        )

    def c_arrival(way, hop, h):
        source = p_source(way, hop) + 1 - 2 * core
        here = p_slice(source, h)
        return pltpu.make_async_copy(here, here, c_recv.at[way, hop, h])

    def travels(way, hop):
        if hop < far:
            return (0, 1) if way == 0 else (1, 0)
        return (way,) if hop == far else ()

    pieces = [
        (way, hop, travels(way, hop)[place])
        for hop in range(1, far + 1)
        for place in range(len(travels(0, hop)))
        for way in range(2)
    ]
    shared = [(0, 0, 0), (0, 0, 1)] + pieces

    def take(way, hop, h):
        r_arrival(way, hop, h).wait()
        if h in travels(way, hop + 1):
            r_copy(way, hop + 1, h).start()
        c_copy(way, hop, h).start()

    def turn_first(k):
        f_copy(k).wait()
        rows = pl.ds(k * size, size)
        first_all[rows, :, own_q] = jnp.swapaxes(first_all[rows, :, own_q], 0, 1)

    def turn_block(k):
        t_copy(k).wait()
        slot = slot_of(k)

        def turn(i, _):
            held[slot, i] = jnp.swapaxes(held[slot, i], 0, 1)
            return 0

        lax.fori_loop(0, groups, turn, 0)

    for k in range(chunks):
        f_copy(k).start()
    own_second.start()
    pl.semaphore_wait(barrier, ncol + ndev - 2)
    for way, hop, h in pieces:
        if hop == 1:
            r_copy(way, 1, h).start()
    for h in range(2):
        c_copy(0, 0, h).start()
    ahead = chunks - 2
    for k in range(chunks):
        turn_first(k)
        if k < ahead:
            z_own(k)
    for k in range(chunks - 1):
        t_copy(k).start()

    width = n_a * n_b
    rows = lax.broadcasted_iota(jnp.int32, (width, width), 0)
    columns = lax.broadcasted_iota(jnp.int32, (width, width), 1)
    order[...] = (rows == lax.rem(columns, n_b) * n_a + lax.div(columns, n_b)).astype(jnp.bfloat16)

    def take_hop(want, place):
        for way in range(2):
            if place < len(travels(way, want)):
                take(way, want, travels(way, want)[place])

    def z_relays(k, hops):
        for hop in hops:
            z_relay(hop, k, False if hop == 1 else None)

    def z_prompt(blocks):
        if ndev > 2:
            for k in blocks:
                z_relay(1, k, True)

    further = range(2, ndev - 1)
    for k in range(min(2, chunks - 1)):
        turn_block(k)
        if ndev > 2:
            z_relay(1, k)
        z_own(ahead + k)
    for k in range(2, chunks - 1):
        turn_block(k)
    total[...] = jnp.zeros_like(total)
    half = 2 + (chunks - 2) // 2
    take_hop(1, 0)
    z_prompt(range(2, half))
    z_relays(0, further)
    take_hop(1, 1)
    z_prompt(range(half, chunks))
    z_relays(1, further)
    for k in range(2, EARLY):
        z_relays(k, range(1, ndev - 1))
    for hop in range(2, far + 1):
        for place in range(len(travels(0, hop))):
            take_hop(hop, place)
    own_second.wait()
    for piece in shared:
        c_arrival(*piece).wait()

    def rows_of(k):
        return pl.ds(k * size, size)

    def product(k, b, columns):
        left = first_all[rows_of(k), :, columns].reshape(size * n_a, -1)
        right = second_all[pl.ds(b * WIDE, WIDE), :, columns].reshape(WIDE * n_d, -1)
        return lax.dot_general(left, right, NT, preferred_element_type=jnp.float32)

    def keep(b, got):
        got = got.astype(jnp.bfloat16)
        for i in range(WIDE):
            tile[:, b * WIDE + i] = got[:, i * n_d : (i + 1) * n_d].reshape(size, n_a, n_d)

    def contract(k):
        slot = slot_of(k)

        def some_c(g, _):
            group = [g * GROUP + i for i in range(GROUP)]
            left = jnp.concatenate([held[slot, :, c].reshape(pairs, n_d) for c in group], axis=1)
            right = jnp.concatenate([tile[c].reshape(n_b * n_a, n_d) for c in group], axis=1)
            got = lax.dot_general(left, right, NT, preferred_element_type=jnp.float32)
            total[...] += got.reshape(total.shape)
            return 0

        lax.fori_loop(0, size // GROUP, some_c, 0)

    everything = pl.ds(0, ndev * q_first)

    def one_block(k, _):
        z_need(k, range(1, ndev))

        def one_b(b, _):
            keep(b, product(k, b, everything))
            return 0

        lax.fori_loop(0, n_b // WIDE, one_b, 0)

        @pl.when(k + EARLY < chunks)
        def _():
            z_relays(k + EARLY, range(1, ndev - 1))

        contract(k)

        @pl.when(k == 0)
        def _():
            t_copy(chunks - 1).start()

        @pl.when(k == 1)
        def _():
            turn_block(chunks - 1)

        return 0

    lax.fori_loop(0, chunks - 1, one_block, 0)

    end = chunks - 1
    low = dev * 2 < ndev
    piece_q = q_first // 2

    def last_q(share):
        start = jnp.where(low, ndev - 1, 0) * q_first + share * piece_q
        return pl.ds(pl.multiple_of(start, piece_q), piece_q)

    others = pl.ds(pl.multiple_of(jnp.where(low, 0, q_first), q_first), (ndev - 1) * q_first)
    z_need(end, range(1, ndev - 1))

    def early_b(b, _):
        carry[b] = product(end, b, others)
        return 0

    lax.fori_loop(0, n_b // WIDE, early_b, 0)
    z_need(end, range(ndev - 1, ndev), (0,))

    def middle_b(b, _):
        carry[b] += product(end, b, last_q(0))
        return 0

    lax.fori_loop(0, n_b // WIDE, middle_b, 0)
    z_need(end, range(ndev - 1, ndev), (1,))

    def late_b(b, _):
        keep(b, carry[b] + product(end, b, last_q(1)))
        return 0

    lax.fori_loop(0, n_b // WIDE, late_b, 0)

    targets = [jnp.where(low, ndev - 1 - i, i) for i in range(ndev)]
    per_chip = groups // chips
    per_core = per_chip // 2

    def contract_side(side):
        slot = slot_of(end)

        def some_c(g, _):
            group = [g * GROUP + i for i in range(GROUP)]
            left = jnp.concatenate([
                jnp.concatenate([
                    held[slot, pl.ds(i * per_chip + side * per_core, per_core), c].reshape(-1, n_d)
                    for i in range(chips)
                ], axis=0)
                for c in group
            ], axis=1)
            right = jnp.concatenate([tile[c].reshape(n_b * n_a, n_d) for c in group], axis=1)
            got = lax.dot_general(left, right, NT, preferred_element_type=jnp.float32)
            total[:, side] += got.reshape(mate.shape)
            return 0

        lax.fori_loop(0, size // GROUP, some_c, 0)

    def x_copy(place):
        target = targets[place]
        return pltpu.make_async_remote_copy(
            src_ref=total.at[:, 1 - core, target],
            dst_ref=mate.at[:, target],
            send_sem=x_send.at[place],
            recv_sem=x_recv.at[place],
            device_id={"col": partner},
            device_id_type=MESH,
        )

    def s_copy(off, place):
        to, target = lax.rem(chip + off, chips), targets[place]
        return pltpu.make_async_remote_copy(
            src_ref=joined.at[to, target],
            dst_ref=parts.at[off, target],
            send_sem=s_send.at[off, place],
            recv_sem=s_recv.at[off, place],
            device_id={"col": to * 2 + core},
            device_id_type=MESH,
        )

    def d_copy(target):
        return pltpu.make_async_remote_copy(
            src_ref=half_sum.at[target],
            dst_ref=final.at[dev],
            send_sem=d_send.at[target],
            recv_sem=d_recv.at[dev],
            device_id={"dev": target},
            device_id_type=MESH,
        )

    contract_side(1 - core)
    for place in range(ndev):
        x_copy(place).start()
    contract_side(core)
    for place in range(ndev):
        target = targets[place]
        x_copy(place).wait_recv()
        joined[:, target] = total[:, core, target] + mate[:, target]
        for off in range(1, chips):
            s_copy(off, place).start()
    for piece in pieces:
        r_copy(*piece).wait_send()
    for piece in shared:
        c_copy(*piece).wait_send()

    def drain(k, _):
        for way in range(2):
            for hop in range(1, ndev):
                @pl.when(sends(way, hop))
                def _():
                    for copy in z_copies(way, hop, k):
                        copy.wait_send()
        return 0

    lax.fori_loop(0, chunks, drain, 0)

    for place in range(ndev):
        target = targets[place]
        mine = joined[chip, target]
        for off in range(1, chips):
            s_copy(off, place).wait_recv()
            mine += parts[off, target]
        half_sum[target] = mine

        @pl.when(target != dev)
        def _():
            d_copy(target).start()

    result = half_sum[dev]
    for off in range(1, ndev):
        source = lax.rem(dev + off, ndev)
        pltpu.make_async_copy(final.at[source], final.at[source], d_recv.at[source]).wait()
        result += final[source]
    high = result.astype(jnp.bfloat16)
    result -= high.astype(jnp.float32)
    middle = result.astype(jnp.bfloat16)
    result -= middle.astype(jnp.float32)
    split = (high, middle, result.astype(jnp.bfloat16))
    moved = [jnp.dot(part, order[...], preferred_element_type=jnp.float32) for part in split]
    out[...] = moved[0] + moved[1] + moved[2]

    for place in range(ndev):
        x_copy(place).wait_send()
        for off in range(1, chips):
            s_copy(off, place).wait_send()
    for off in range(1, ndev):
        d_copy(lax.rem(dev + off, ndev)).wait_send()


def on_device(ncol, ndev, first_factor, second_factor, amplitudes):
    n_a, n_c, q_first = first_factor.shape
    n_b, n_d, q_second = second_factor.shape
    pairs = amplitudes.shape[0]
    groups = pairs // BLOCK
    size = n_a
    chunks = n_c // size
    chips = ncol // 2
    far = chips // 2
    whole = q_first * ndev
    some = pairs // ncol
    few = some // ndev
    width = n_a * n_b
    anywhere = pl.BlockSpec(memory_space=pl.ANY)
    dma = pltpu.SemaphoreType.DMA
    return pl.pallas_call(
        functools.partial(kernel, ncol, ndev),
        out_shape=jax.ShapeDtypeStruct((few, width), jnp.float32),
        in_specs=[anywhere] * 3,
        out_specs=pl.BlockSpec(memory_space=pltpu.VMEM),
        scratch_shapes=[
            pltpu.VMEM((n_c, n_a, whole), jnp.bfloat16),
            pltpu.VMEM((n_b, n_d, whole), jnp.bfloat16),
            pltpu.VMEM((n_c // BLOCK - 1, groups, BLOCK, BLOCK, n_d), jnp.bfloat16),
            pltpu.VMEM((size, n_b, n_a, n_d), jnp.bfloat16),
            pltpu.VMEM((n_b // WIDE, size * n_a, WIDE * n_d), jnp.float32),
            pltpu.VMEM((width, width), jnp.bfloat16),
            pltpu.VMEM((chips, 2, ndev, few, width), jnp.float32),
            pltpu.VMEM((chips, ndev, few, width), jnp.float32),
            pltpu.VMEM((chips, ndev, few, width), jnp.float32),
            pltpu.VMEM((chips, ndev, few, width), jnp.float32),
            pltpu.VMEM((ndev, few, width), jnp.float32),
            pltpu.VMEM((ndev, few, width), jnp.float32),
            dma((chunks,)),
            dma((1,)),
            dma((2, ndev - 1, chunks, 2)),
            dma((2, ndev - 1, chunks, 2)),
            dma((2, far, 2)),
            dma((2, far, 2)),
            dma((2, far + 1, 2)),
            dma((2, far + 1, 2)),
            dma((n_c // BLOCK,)),
            dma((ndev,)),
            dma((ndev,)),
            dma((chips, ndev)),
            dma((chips, ndev)),
            dma((ndev,)),
            dma((ndev,)),
        ],
        compiler_params=pltpu.CompilerParams(
            collective_id=0, has_side_effects=True, vmem_limit_bytes=67043328
        ),
    )(first_factor, second_factor, amplitudes.reshape(groups, BLOCK, n_c, n_d))


def solution(mesh):
    placed = (P(None, "col", "dev"), P(None, "dev", "col"), P(None, "col", "dev"))
    return jax.shard_map(
        functools.partial(on_device, mesh.shape["col"], mesh.shape["dev"]),
        mesh=mesh, in_specs=placed, out_specs=P(("col", "dev"), None), check_vma=False,
    )
```
